256 devices in a mesh: gx: 16 (over x, y_lo, core), col: 16 (over y_hi, z).
Axes of the slice: x: 4, y: 4 (y_hi: 2, y_lo: 2; y = y_hi * 2 + y_lo), z: 8, core: 2. Of those that a mesh axis runs over, the one named last changes fastest.
Arguments:
- field: bfloat16 [32, 32, 128, 256], P('col', 'gx'), may hold values from -6 to 6
- kernel: bfloat16 [64, 32, 3, 3, 3], replicated, may hold values from -0.21875 to 0.21875
- bias: float32 [64], P('col'), may hold values from -3 to 3
- cotangent: bfloat16 [64, 16, 64, 128], P('col', 'gx'), may hold values from -6 to 6
Outputs:
- out_act: bfloat16 [64, 16, 64, 128], P('col', 'gx')
- in_grad: bfloat16 [32, 32, 128, 256], P('col', 'gx')
The draws below stay inside these ranges and needn't reach their ends.
All inputs are finite; a program needn't handle non-finite values.
Results may differ from the reference program's by a relative error of at most 0.014.
Values may be sent and summed in bfloat16 or wider, within the bound.
A program may use at most 128 MiB of HBM per device.

```python
import jax
import jax.numpy as jnp
from jax import lax

CIN = 32
COUT = 64
Y = 128
Z = 256
X = 32


def steps_of(stream_key, extent, pieces, low, high):
    factor_of, own = 1.0, jax.random.fold_in(stream_key, 6)
    for dim, shards_of in pieces:
        draws = jnp.exp(jax.random.uniform(jax.random.fold_in(own, dim), (shards_of,), jnp.float32, low / len(pieces), high / len(pieces)))
        factor_of = factor_of * jnp.repeat(draws, extent[dim] // shards_of).reshape([-1 if axis == dim else 1 for axis in range(len(extent))])
    return factor_of


def bell_draw(stream_key, extent, width, reach, shards=(), kind=jnp.bfloat16):
    gain = steps_of(stream_key, extent, shards, -0.22, 0.18) if shards else 1.0
    values = jax.random.normal(stream_key, extent, jnp.float32) * width * gain
    return jnp.minimum(jnp.maximum(values, -reach), reach).astype(kind)


def setup_inputs(seed: int = 0) -> dict:
    splits = jax.random.split(jax.random.key(seed), 5)
    field = bell_draw(splits[0], (CIN, X, Y, Z), 1.0, 6.0, ((0, 16), (1, 16)))
    kernel = bell_draw(splits[1], (COUT, CIN, 3, 3, 3), (CIN * 27) ** -0.5, 0.21875)
    bias = bell_draw(splits[2], (COUT,), 0.5, 3.0, ((0, 16),), jnp.float32)
    cotangent = bell_draw(splits[3], (COUT, X // 2, Y // 2, Z // 2), 1.0, 6.0, ((0, 16), (1, 16)))
    return dict(field=field, kernel=kernel, bias=bias, cotangent=cotangent)


def periodic_conv(values, kernel_wide):
    padded = jnp.pad(values, ((0, 0), (1, 1), (1, 1), (1, 1)), mode='wrap')
    result = lax.conv_general_dilated(padded[None], kernel_wide, (2, 2, 2), 'VALID', dimension_numbers=('NCDHW', 'OIDHW', 'NCDHW'), precision=lax.Precision.HIGHEST)
    return result[0]

def reference(field, kernel, bias, cotangent):
    kernel_wide = kernel.astype(jnp.float32)
    field_wide = field.astype(jnp.float32)
    pre = periodic_conv(field_wide, kernel_wide) + bias.astype(jnp.float32)[:, None, None, None]
    out_act = (0.3 * pre + 0.7 * jax.nn.softplus(pre)).astype(jnp.bfloat16)
    masked = (cotangent.astype(jnp.float32) * (0.3 + 0.7 * jax.nn.sigmoid(pre))).astype(jnp.bfloat16)

    def forward_map(values):
        return periodic_conv(values, kernel_wide)
    _, pullback = jax.vjp(forward_map, field_wide)
    in_grad, = pullback(masked.astype(jnp.float32))
    return (out_act, in_grad.astype(jnp.bfloat16))
```

```python
import functools

import jax
import jax.numpy as jnp
from jax import lax
from jax.experimental import pallas as pl
from jax.experimental.pallas import tpu as pltpu
from jax.sharding import PartitionSpec as P

F32 = jnp.float32
BF16 = jnp.bfloat16
MESH = pl.DeviceIdType.MESH

X1, X0, CT, BS, OS, G0, G1, XH, H1, HM, H0, M1, N0, N1 = range(14)
KINDS = 14


def iota(shape, dim):
    return lax.broadcasted_iota(jnp.int32, shape, dim)


def one_hot(hit):
    return jnp.where(hit, 1.0, 0.0).astype(BF16)


def dot(a, b):
    return jnp.dot(a, b, preferred_element_type=F32)


def row_block(position, ranks):
    return position + (position // (ranks // 2)) * (3 * ranks // 2 - 1 - 2 * position)


def block_kernel(
    slabs, ranks,
    field, wt, bias, cot,
    act, grad,
    rx1, rx0, rxh, h1, h0, hm, hs1, hs0,
    cs, crx, bs, brx, outs, orx, m0, m1, tg0, tg1,
    tf, tt, sel, send, recv,
):
    slab = lax.axis_index("gx")
    me = lax.axis_index("col")
    block = row_block(me, ranks)
    above = lax.rem(slab + 1, slabs)
    below = lax.rem(slab + slabs - 1, slabs)
    after = row_block(lax.rem(block + 1, ranks), ranks)
    before = row_block(lax.rem(block + ranks - 1, ranks), ranks)

    barrier = pltpu.get_barrier_semaphore()

    def greet(step, carry):
        peer = lax.rem(me + step, ranks)
        pl.semaphore_signal(barrier, inc=1, device_id=(slab, peer), device_id_type=MESH)
        return carry

    lax.fori_loop(1, ranks, greet, 0)
    for where in ((above, me), (below, me), (above, after), (below, before)):
        pl.semaphore_signal(barrier, inc=1, device_id=where, device_id_type=MESH)

    def remote(src, dst, kind, where):
        return pltpu.make_async_remote_copy(
            src_ref=src, dst_ref=dst, send_sem=send.at[kind], recv_sem=recv.at[kind],
            device_id=where, device_id_type=MESH,
        )

    def landed(ref, kind):
        pltpu.make_async_copy(ref, ref, recv.at[kind]).wait()

    def left(ref, kind):
        pltpu.make_async_copy(ref, ref, send.at[kind]).wait()

    def scatter(kind, source, target):
        def one(step, carry):
            peer = lax.rem(me + step, ranks)
            remote(source(peer), target, kind, (slab, peer)).start()
            return carry

        lax.fori_loop(1, ranks, one, 0)
        pltpu.make_async_copy(source(me), target, recv.at[kind]).start()

    to = iota((256, 256), 0)
    frm = iota((256, 256), 1)
    order = one_hot(frm == (to % 4) * 64 + (to // 16) * 4 + (to // 4) % 4)
    cs[...] = dot(order, cot[...]).astype(BF16).reshape(ranks, 16, 128)
    bs[...] = jnp.zeros(bs.shape, F32)
    bs[0:1, 0:4] = bias[...]
    source_z = iota((256, 384), 0)
    tap = iota((256, 384), 1)
    sel[...] = one_hot(source_z == (2 * (tap % 128) + tap // 128 + 255) % 256)

    pl.semaphore_wait(barrier, ranks - 1 + 4)

    scatter(X1, lambda peer: field.at[:, 1, row_block(peer, ranks)], rx1.at[me])
    scatter(X0, lambda peer: field.at[:, 0, row_block(peer, ranks)], rx0.at[me])
    scatter(CT, lambda peer: cs.at[row_block(peer, ranks)], crx.at[me])
    scatter(BS, lambda peer: bs, brx.at[me])

    spread_t = one_hot(iota((32, 256), 0) == iota((32, 256), 1) // 8)
    spread = one_hot(iota((256, 32), 1) == iota((256, 32), 0) // 8)
    row_f = iota((64, 256), 1) % 8
    row_t = iota((256, 128), 0) % 8
    half_t = iota((256, 128), 1) // 64

    def pick(gap, parts):
        return jnp.where(
            gap == 0, parts[0], jnp.where(gap == 1, parts[1], jnp.where(gap == 2, parts[2], 0.0))
        ).astype(BF16)

    def build(index, carry):
        a = index // 3
        e = index % 3
        taps = [wt[a, b, e] for b in range(3)]
        wide = [
            lax.dot_general(w, spread_t, (((0,), (0,)), ((), ())), preferred_element_type=F32)
            for w in taps
        ]
        for j in range(4):
            tf[index, 64 * j : 64 * j + 64, :] = pick(row_f - 2 * j + 1, wide)
        tall = [dot(spread, jnp.concatenate([w, w], axis=1)) for w in taps]
        for pair in range(3):
            j = 2 * pair + half_t
            gap = jnp.where(j > 4, 9, row_t - 2 * j + 1)
            tt[index, :, 128 * pair : 128 * pair + 128] = pick(gap, tall)
        return carry

    lax.fori_loop(0, 9, build, 0)
    m0[320:384, :] = jnp.zeros((64, 128), BF16)
    m1[320:384, :] = jnp.zeros((64, 128), BF16)

    def split(rows):
        return dot(rows, sel[...]).astype(BF16)

    def rows_of(ref):
        return ref[...].astype(F32).reshape(256, 256).astype(BF16)

    def body_taps(a, views):
        total = dot(tf[3 * a], views[:, 0:128])
        total = total + dot(tf[3 * a + 1], views[:, 128:256])
        return total + dot(tf[3 * a + 2], views[:, 256:384])

    def edge_taps(a, rows):
        views = split(rows)
        total = None
        for e in range(3):
            part = lax.dot_general(
                wt[a, 0, e], views[:, 128 * e : 128 * e + 128],
                (((0,), (0,)), ((), ())), preferred_element_type=F32,
            )
            total = part if total is None else total + part
        return total

    last_row = one_hot(iota((32, 256), 1) == 8 * iota((32, 256), 0) + 7)

    landed(rx1, X1)
    remote(rx1, rxh, XH, (above, me)).start()
    plane = rows_of(rx1)
    hs1[...] = dot(last_row, plane).astype(BF16)
    remote(hs1, h1, H1, (slab, after)).start()
    remote(hs1, hm, HM, (above, after)).start()
    pre = body_taps(2, split(plane))

    landed(rx0, X0)
    plane = rows_of(rx0)
    hs0[...] = dot(last_row, plane).astype(BF16)
    remote(hs0, h0, H0, (slab, after)).start()
    pre = pre + body_taps(1, split(plane))

    landed(brx, BS)
    owner = iota((64, 128), 0) // 4
    shown = jnp.zeros((64, 128), F32)
    for rank in range(ranks):
        shown = jnp.where(owner == rank, jnp.broadcast_to(brx[rank], (64, 128)), shown)
    mine = iota((64, 128), 1) == iota((64, 128), 0) % 4
    column = jnp.sum(jnp.where(mine, shown, 0.0), axis=1, keepdims=True)
    order = one_hot(frm == (to % 64) // 4 * 16 + (to // 64) * 4 + to % 4)
    landed(crx, CT)
    upstream = dot(order, crx[...].reshape(256, 128))

    landed(h1, H1)
    edge = edge_taps(2, h1[...]) + jnp.broadcast_to(column, (64, 128))
    landed(h0, H0)
    edge = edge + edge_taps(1, h0[...])
    landed(hm, HM)
    edge = edge + edge_taps(0, hm[...])
    landed(rxh, XH)
    pre = pre + body_taps(0, split(rows_of(rxh)))
    rest = jnp.broadcast_to(column, (64, 128))
    pre = pre + jnp.concatenate([edge, rest, rest, rest], axis=0)

    decay = jnp.exp(-jnp.abs(pre))
    out = (0.3 * pre + 0.7 * (jnp.maximum(pre, 0.0) + jnp.log1p(decay))).astype(BF16)
    gate = jnp.where(pre >= 0.0, 1.0, decay) / (1.0 + decay)
    masked = (upstream * (0.3 + 0.7 * gate)).astype(BF16)
    m0[0:256, :] = masked
    remote(m0.at[pl.ds(0, 256)], m1.at[pl.ds(0, 256)], M1, (below, me)).start()
    remote(m0.at[pl.ds(0, 64)], m1.at[pl.ds(256, 64)], N1, (below, before)).start()
    remote(m0.at[pl.ds(0, 64)], m0.at[pl.ds(256, 64)], N0, (slab, before)).start()

    order = one_hot(frm == (to // 4) % 4 * 64 + to // 16 * 4 + to % 4)
    outs[...] = dot(order, out).astype(BF16).reshape(ranks, 16, 128)
    scatter(OS, lambda peer: outs.at[peer], orx.at[block])

    weave = one_hot(frm // 2 + (frm % 2) * 128 == to)

    def woven(even, odd):
        both = jnp.concatenate([even.astype(BF16), odd.astype(BF16)], axis=1)
        return dot(both, weave).astype(BF16).reshape(ranks, 2, 8, 256)

    def moved(rows):
        return pltpu.roll(rows.astype(F32), 127, 1).astype(BF16)

    landed(m0.at[pl.ds(256, 64)], N0)
    here = m0[...]
    here_next = moved(here)
    tg0[...] = woven(dot(tt[4], here), dot(tt[5], here) + dot(tt[3], here_next))
    scatter(G0, lambda peer: tg0.at[peer], grad.at[:, 0, block])
    even = dot(tt[7], here)
    odd = dot(tt[8], here) + dot(tt[6], here_next)
    landed(m1.at[pl.ds(0, 256)], M1)
    landed(m1.at[pl.ds(256, 64)], N1)
    there = m1[...]
    tg1[...] = woven(even + dot(tt[1], there), odd + dot(tt[2], there) + dot(tt[0], moved(there)))
    scatter(G1, lambda peer: tg1.at[peer], grad.at[:, 1, block])

    landed(orx, OS)
    order = one_hot(frm == (to % 64) // 4 * 16 + (to % 4) * 4 + to // 64)
    act[...] = dot(order, orx[...].reshape(256, 128)).astype(BF16)

    others = pl.ds(0, ranks - 1)
    for ref, kind in (
        (rx1.at[others], X1), (rx0.at[others], X0), (crx.at[others], CT), (brx.at[others], BS),
        (outs.at[others], OS), (tg0.at[others], G0), (tg1.at[others], G1),
        (rx1, XH), (hs1, H1), (hs1, HM), (hs0, H0),
        (m0.at[pl.ds(0, 256)], M1), (m0.at[pl.ds(0, 64)], N1), (m0.at[pl.ds(0, 64)], N0),
    ):
        left(ref, kind)
    landed(grad.at[:, 0], G0)
    landed(grad.at[:, 1], G1)


def on_device(slabs, ranks, field, kernel, bias, cotangent):
    vmem = pl.BlockSpec(memory_space=pltpu.VMEM)
    call = pl.pallas_call(
        functools.partial(block_kernel, slabs, ranks),
        out_shape=(
            jax.ShapeDtypeStruct((256, 128), BF16),
            jax.ShapeDtypeStruct((2, 2, ranks, 8, 256), BF16),
        ),
        in_specs=[vmem] * 4,
        out_specs=(vmem, vmem),
        scratch_shapes=[
            pltpu.VMEM((ranks, 2, 8, 256), BF16),
            pltpu.VMEM((ranks, 2, 8, 256), BF16),
            pltpu.VMEM((ranks, 2, 8, 256), BF16),
            pltpu.VMEM((32, 256), BF16),
            pltpu.VMEM((32, 256), BF16),
            pltpu.VMEM((32, 256), BF16),
            pltpu.VMEM((32, 256), BF16),
            pltpu.VMEM((32, 256), BF16),
            pltpu.VMEM((ranks, 16, 128), BF16),
            pltpu.VMEM((ranks, 16, 128), BF16),
            pltpu.VMEM((1, 128), F32),
            pltpu.VMEM((ranks, 1, 128), F32),
            pltpu.VMEM((ranks, 16, 128), BF16),
            pltpu.VMEM((ranks, 16, 128), BF16),
            pltpu.VMEM((384, 128), BF16),
            pltpu.VMEM((384, 128), BF16),
            pltpu.VMEM((ranks, 2, 8, 256), BF16),
            pltpu.VMEM((ranks, 2, 8, 256), BF16),
            pltpu.VMEM((9, 256, 256), BF16),
            pltpu.VMEM((9, 256, 384), BF16),
            pltpu.VMEM((256, 384), BF16),
            pltpu.SemaphoreType.DMA((KINDS,)),
            pltpu.SemaphoreType.DMA((KINDS,)),
        ],
        compiler_params=pltpu.CompilerParams(collective_id=0, has_side_effects=True),
        name="row_blocks",
    )
    act, grad = call(
        field.reshape(2, 2, ranks, 8, 256),
        kernel.transpose(2, 3, 4, 1, 0),
        bias.reshape(1, 4),
        cotangent.reshape(256, 128),
    )
    return act.reshape(4, 1, 64, 128), grad.reshape(2, 2, 128, 256)


def solution(mesh):
    in_specs = (P("col", "gx", None, None), P(), P("col"), P("col", "gx", None, None))
    out_specs = (P("col", "gx", None, None), P("col", "gx", None, None))
    return jax.shard_map(
        functools.partial(on_device, mesh.shape["gx"], mesh.shape["col"]),
        mesh=mesh, in_specs=in_specs, out_specs=out_specs, check_vma=False,
    )
```

```python
import functools

import jax
import jax.numpy as jnp
from jax import lax
from jax.experimental import pallas as pl
from jax.experimental.pallas import tpu as pltpu
from jax.sharding import PartitionSpec as P

F32 = jnp.float32
BF16 = jnp.bfloat16
MESH = pl.DeviceIdType.MESH

X1, X0, CT, BS, OS, G0, G1, XH, H1, HM, H0, L1, LM, L0, M1 = range(15)
KINDS = 15


def iota(shape, dim):
    return lax.broadcasted_iota(jnp.int32, shape, dim)


def one_hot(hit):
    return jnp.where(hit, 1.0, 0.0).astype(BF16)


def dot(a, b):
    return jnp.dot(a, b, preferred_element_type=F32)


def row_block(position, ranks):
    return position + (position // (ranks // 2)) * (3 * ranks // 2 - 1 - 2 * position)


def block_kernel(
    slabs, ranks,
    field, wt_hbm, bias_hbm, cot_hbm,
    orx, grad,
    rx1, rx0, rxh, h1, h0, hm, hs1, hs0,
    wt, bias, cot, cs, crx, bs, brx, outs, m0, m1, tg0, tg1,
    tf, tt, sel, send, recv, load,
):
    slab = lax.axis_index("gx")
    me = lax.axis_index("col")
    block = row_block(me, ranks)
    above = lax.rem(slab + 1, slabs)
    below = lax.rem(slab + slabs - 1, slabs)
    after = row_block(lax.rem(block + 1, ranks), ranks)
    before = row_block(lax.rem(block + ranks - 1, ranks), ranks)

    barrier = pltpu.get_barrier_semaphore()

    def peer_of(step):
        turn = step // 2
        z = me + ranks // 4 + (1 - 2 * (turn % 2)) * ((turn + 1) // 2)
        y = me // (ranks // 2) + 1 - step % 2
        return (z % (ranks // 2)) + (y % 2) * (ranks // 2)

    def greet(step, carry):
        peer = peer_of(step)
        pl.semaphore_signal(barrier, inc=1, device_id=(slab, peer), device_id_type=MESH)
        return carry

    lax.fori_loop(0, ranks - 1, greet, 0)
    for where in (
        (above, me), (below, me), (above, after), (below, before), (above, before), (below, after)
    ):
        pl.semaphore_signal(barrier, inc=1, device_id=where, device_id_type=MESH)

    def remote(src, dst, kind, where):
        return pltpu.make_async_remote_copy(
            src_ref=src, dst_ref=dst, send_sem=send.at[kind], recv_sem=recv.at[kind],
            device_id=where, device_id_type=MESH,
        )

    def landed(ref, kind):
        pltpu.make_async_copy(ref, ref, recv.at[kind]).wait()

    def left(ref, kind):
        pltpu.make_async_copy(ref, ref, send.at[kind]).wait()

    def scatter(kind, source, target):
        def one(step, carry):
            peer = peer_of(step)
            remote(source(peer), target, kind, (slab, peer)).start()
            return carry

        lax.fori_loop(0, ranks - 1, one, 0)
        pltpu.make_async_copy(source(me), target, recv.at[kind]).start()

    loads = [
        pltpu.make_async_copy(src, dst, load.at[slot])
        for slot, (src, dst) in enumerate(((cot_hbm, cot), (bias_hbm, bias), (wt_hbm, wt)))
    ]
    for copy in loads:
        copy.start()
    bs[...] = jnp.zeros(bs.shape, F32)

    pl.semaphore_wait(barrier, ranks - 1 + 6)

    scatter(X1, lambda peer: field.at[:, 1, row_block(peer, ranks)], rx1.at[me])
    scatter(X0, lambda peer: field.at[:, 0, row_block(peer, ranks)], rx0.at[me])

    to = iota((384, 256), 0)
    frm = iota((384, 256), 1)
    taken = to % 24
    wanted = (taken % 4) * 64 + (to // 24 * 4 + taken // 4) % 64
    order = one_hot((frm == wanted) & (taken < 20))
    loads[0].wait()
    cs[...] = dot(order, cot[...]).reshape(ranks, 24, 128).astype(BF16)
    scatter(CT, lambda peer: cs.at[row_block(peer, ranks)], crx.at[me])
    loads[1].wait()
    bs[0:1, 0:4] = bias[...]
    scatter(BS, lambda peer: bs, brx.at[me])

    to = iota((256, 256), 0)
    frm = iota((256, 256), 1)
    source_z = iota((256, 384), 0)
    tap = iota((256, 384), 1)
    sel[...] = one_hot(source_z == (2 * (tap % 128) + tap // 128 + 255) % 256)
    loads[2].wait()

    spread_t = one_hot(iota((32, 256), 0) == iota((32, 256), 1) // 8)
    spread = one_hot(iota((256, 32), 1) == iota((256, 32), 0) // 8)
    row_f = iota((64, 256), 1) % 8
    row_t = iota((256, 128), 0) % 8
    half_t = iota((256, 128), 1) // 64

    def pick(gap, parts):
        return jnp.where(
            gap == 0, parts[0], jnp.where(gap == 1, parts[1], jnp.where(gap == 2, parts[2], 0.0))
        ).astype(BF16)

    def build(index, carry):
        a = index // 3
        e = index % 3
        taps = [wt[a, b, e] for b in range(3)]
        wide = [
            lax.dot_general(w, spread_t, (((0,), (0,)), ((), ())), preferred_element_type=F32)
            for w in taps
        ]
        for j in range(5):
            tf[index, 64 * j : 64 * j + 64, :] = pick(row_f - 2 * j + 1, wide)
        tall = [dot(spread, jnp.concatenate([w, w], axis=1)) for w in taps]
        for pair in range(3):
            j = 2 * pair + half_t
            gap = jnp.where(j > 4, 9, row_t - 2 * j + 1)
            tt[index, :, 128 * pair : 128 * pair + 128] = pick(gap, tall)
        return carry

    lax.fori_loop(0, 9, build, 0)
    m0[320:384, :] = jnp.zeros((64, 128), BF16)
    m1[320:384, :] = jnp.zeros((64, 128), BF16)

    def split(rows):
        return dot(rows, sel[...]).astype(BF16)

    def rows_of(ref):
        return ref[...].astype(F32).reshape(256, 256).astype(BF16)

    def body_taps(a, views):
        total = dot(tf[3 * a], views[:, 0:128])
        total = total + dot(tf[3 * a + 1], views[:, 128:256])
        return total + dot(tf[3 * a + 2], views[:, 256:384])

    def edge_taps(a, rows, taps):
        views = split(rows)
        total = None
        for place, b in enumerate(taps):
            for e in range(3):
                part = lax.dot_general(
                    wt[a, b, e], views[32 * place : 32 * place + 32, 128 * e : 128 * e + 128],
                    (((0,), (0,)), ((), ())), preferred_element_type=F32,
                )
                total = part if total is None else total + part
        return total

    edge_row = iota((96, 256), 0)
    edges = one_hot(iota((96, 256), 1) == 8 * (edge_row % 32) + (edge_row // 32 + 7) % 8)
    low, high = pl.ds(0, 32), pl.ds(32, 64)

    landed(rx1, X1)
    remote(rx1, rxh, XH, (above, me)).start()
    plane = rows_of(rx1)
    hs1[...] = dot(edges, plane).astype(BF16)
    remote(hs1.at[low], hm.at[low], HM, (above, after)).start()
    remote(hs1.at[high], hm.at[high], LM, (above, before)).start()
    remote(hs1.at[low], h1.at[low], H1, (slab, after)).start()
    remote(hs1.at[high], h1.at[high], L1, (slab, before)).start()
    pre = body_taps(2, split(plane))

    landed(rx0, X0)
    plane = rows_of(rx0)
    hs0[...] = dot(edges, plane).astype(BF16)
    remote(hs0.at[low], h0.at[low], H0, (slab, after)).start()
    remote(hs0.at[high], h0.at[high], L0, (slab, before)).start()
    pre = pre + body_taps(1, split(plane))

    landed(brx, BS)
    owner = iota((64, 128), 0) // 4
    shown = jnp.zeros((64, 128), F32)
    for rank in range(ranks):
        shown = jnp.where(owner == rank, jnp.broadcast_to(brx[rank], (64, 128)), shown)
    mine = iota((64, 128), 1) == iota((64, 128), 0) % 4
    column = jnp.sum(jnp.where(mine, shown, 0.0), axis=1, keepdims=True)
    dest = iota((320, 384), 0)
    order = one_hot(iota((320, 384), 1) == dest % 64 // 4 * 24 + dest // 64 * 4 + dest % 4)
    landed(crx, CT)
    upstream = dot(order, crx[...].astype(F32).reshape(24 * ranks, 128).astype(BF16))

    rest = jnp.broadcast_to(column, (64, 128))
    first, last = rest, rest
    for ref, a, kinds in ((h1, 2, (H1, L1)), (h0, 1, (H0, L0)), (hm, 0, (HM, LM))):
        landed(ref.at[low], kinds[0])
        landed(ref.at[high], kinds[1])
        first = first + edge_taps(a, ref[0:32, :], (0,))
        last = last + edge_taps(a, ref[32:96, :], (1, 2))
    landed(rxh, XH)
    pre = pre + body_taps(0, split(rows_of(rxh)))
    pre = pre + jnp.concatenate([first, rest, rest, rest, last], axis=0)

    decay = jnp.exp(-jnp.abs(pre))
    out = (0.3 * pre + 0.7 * (jnp.maximum(pre, 0.0) + jnp.log1p(decay))).astype(BF16)
    gate = jnp.where(pre >= 0.0, 1.0, decay) / (1.0 + decay)
    masked = (upstream * (0.3 + 0.7 * gate)).astype(BF16)
    m0[0:320, :] = masked
    whole = pl.ds(0, 320)
    remote(m0.at[whole], m1.at[whole], M1, (below, me)).start()

    weave = one_hot(frm // 2 + (frm % 2) * 128 == to)

    def woven(even, odd):
        both = jnp.concatenate([even.astype(BF16), odd.astype(BF16)], axis=1)
        return dot(both, weave).astype(BF16).reshape(ranks, 2, 8, 256)

    def moved(rows):
        return pltpu.roll(rows.astype(F32), 127, 1).astype(BF16)

    here = m0[...]
    here_next = moved(here)
    tg0[...] = woven(dot(tt[4], here), dot(tt[5], here) + dot(tt[3], here_next))
    scatter(G0, lambda peer: tg0.at[peer], grad.at[:, 0, block])
    order = one_hot(frm == (to // 4) % 4 * 64 + to // 16 * 4 + to % 4)
    outs[...] = dot(order, out[0:256]).astype(BF16).reshape(ranks, 16, 128)
    scatter(OS, lambda peer: outs.at[peer], orx.at[block])

    even = dot(tt[7], here)
    odd = dot(tt[8], here) + dot(tt[6], here_next)
    landed(m1.at[whole], M1)
    there = m1[...]
    tg1[...] = woven(even + dot(tt[1], there), odd + dot(tt[2], there) + dot(tt[0], moved(there)))
    scatter(G1, lambda peer: tg1.at[peer], grad.at[:, 1, block])

    others = pl.ds(0, ranks - 1)
    for ref, kind in (
        (rx1.at[others], X1), (rx0.at[others], X0), (crx.at[others], CT), (brx.at[others], BS),
        (outs.at[others], OS), (tg0.at[others], G0), (tg1.at[others], G1),
        (rx1, XH), (hs1.at[low], H1), (hs1.at[low], HM), (hs0.at[low], H0),
        (hs1.at[high], L1), (hs1.at[high], LM), (hs0.at[high], L0), (m0.at[whole], M1),
    ):
        left(ref, kind)
    landed(orx, OS)
    landed(grad.at[:, 0], G0)
    landed(grad.at[:, 1], G1)


def leave_kernel(orx_hbm, grad_hbm, act_out, grad_out, orx, act, grad, sems):
    reads = [pltpu.make_async_copy(orx_hbm, orx, sems.at[0])]
    writes = []
    for half in range(2):
        reads.append(pltpu.make_async_copy(grad_hbm.at[half], grad.at[half], sems.at[1 + half]))
        writes.append(pltpu.make_async_copy(grad.at[half], grad_out.at[half], sems.at[3 + half]))
    for copy in reads:
        copy.start()
    to = iota((256, 256), 0)
    order = one_hot(iota((256, 256), 1) == (to % 64) // 4 * 16 + (to % 4) * 4 + to // 64)
    reads[0].wait()
    act[...] = dot(order, orx[...].reshape(256, 128)).astype(BF16)
    last = pltpu.make_async_copy(act, act_out, sems.at[5])
    last.start()
    for half in range(2):
        reads[1 + half].wait()
        writes[half].start()
    for copy in writes:
        copy.wait()
    last.wait()


def on_device(slabs, ranks, field, kernel, bias, cotangent):
    where = pl.BlockSpec(memory_space=pl.ANY)
    block = pltpu.VMEM((ranks, 2, 8, 256), BF16)
    edge = pltpu.VMEM((96, 256), BF16)
    act_shape = jax.ShapeDtypeStruct((ranks, 16, 128), BF16)
    grad_shape = jax.ShapeDtypeStruct((2, 2, ranks, 8, 256), BF16)
    call = pl.pallas_call(
        functools.partial(block_kernel, slabs, ranks),
        out_shape=(act_shape, grad_shape),
        in_specs=[where] * 4,
        out_specs=(where, where),
        scratch_shapes=[
            block, block, block,
            edge, edge, edge, edge, edge,
            pltpu.VMEM((3, 3, 3, 32, 64), BF16),
            pltpu.VMEM((1, 4), F32),
            pltpu.VMEM((256, 128), BF16),
            pltpu.VMEM((ranks, 24, 128), BF16),
            pltpu.VMEM((ranks, 24, 128), BF16),
            pltpu.VMEM((1, 128), F32),
            pltpu.VMEM((ranks, 1, 128), F32),
            pltpu.VMEM((ranks, 16, 128), BF16),
            pltpu.VMEM((384, 128), BF16),
            pltpu.VMEM((384, 128), BF16),
            block, block,
            pltpu.VMEM((9, 320, 256), BF16),
            pltpu.VMEM((9, 256, 384), BF16),
            pltpu.VMEM((256, 384), BF16),
            pltpu.SemaphoreType.DMA((KINDS,)),
            pltpu.SemaphoreType.DMA((KINDS,)),
            pltpu.SemaphoreType.DMA((3,)),
        ],
        compiler_params=pltpu.CompilerParams(collective_id=0, has_side_effects=True),
        name="row_blocks",
    )
    orx, grad = call(
        field.reshape(2, 2, ranks, 8, 256),
        kernel.transpose(2, 3, 4, 1, 0),
        bias.reshape(1, 4),
        cotangent.reshape(256, 128),
    )
    leave = pl.pallas_call(
        leave_kernel,
        out_shape=(jax.ShapeDtypeStruct((256, 128), BF16), grad_shape),
        in_specs=[where] * 2,
        out_specs=(where, where),
        scratch_shapes=[
            pltpu.VMEM((ranks, 16, 128), BF16),
            pltpu.VMEM((256, 128), BF16),
            pltpu.VMEM((2, 2, ranks, 8, 256), BF16),
            pltpu.SemaphoreType.DMA((6,)),
        ],
        name="leave",
    )
    act, grad = leave(orx, grad)
    return act.reshape(4, 1, 64, 128), grad.reshape(2, 2, 128, 256)


def solution(mesh):
    in_specs = (P("col", "gx", None, None), P(), P("col"), P("col", "gx", None, None))
    out_specs = (P("col", "gx", None, None), P("col", "gx", None, None))
    return jax.shard_map(
        functools.partial(on_device, mesh.shape["gx"], mesh.shape["col"]),
        mesh=mesh, in_specs=in_specs, out_specs=out_specs, check_vma=False,
    )
```
